32 devices in a mesh: row: 4 (over y, core), col: 8 (over z, x).
Axes of the slice: x: 2, y: 2, z: 4, core: 2. Of those that a mesh axis runs over, the one named last changes fastest.
Arguments:
- pair: bfloat16 [1024, 1024, 128], P('row', 'col'), may hold values from -6 to 6
- norm_gain: float32 [128], replicated, may hold values from 0.1 to 1.9
- norm_shift: float32 [128], replicated, may hold values from -3 to 3
- w_query: bfloat16 [128, 128], replicated, may hold values from -1 to 1
- w_key: bfloat16 [128, 128], replicated, may hold values from -0.5 to 0.5
- w_value: bfloat16 [128, 128], replicated, may hold values from -0.5 to 0.5
- w_gate: bfloat16 [128, 128], replicated, may hold values from -0.5 to 0.5
- gate_shift: float32 [128], replicated, may hold values from -1 to 1
- w_bias: float32 [128, 4], replicated, may hold values from -30 to 30
- w_out: bfloat16 [128, 128], replicated, may hold values from -1 to 1
- out_shift: float32 [128], replicated, may hold values from -3 to 3
Outputs:
- update: bfloat16 [1024, 1024, 128], P('row', 'col')
The draws below stay inside these ranges and needn't reach their ends.
All inputs are finite; a program needn't handle non-finite values.
Results may differ from the reference program's by a relative error of at most 0.0015.
The reference program's roundings to bfloat16 on the way (of `normed`, `query`, `weights` and `gated`) count: a program that leaves them out, or rounds other values in their place, can miss the bound.
Values may be sent and summed in bfloat16 or wider, within the bound.
A program may use at most 128 MiB of HBM per device.

```python
import math
import jax
import jax.numpy as jnp
from jax import lax

N = 1024
C = 128
H = 4
DH = 32


def draw_w_bias(key, part):
    first, second = jax.random.split(jax.random.fold_in(key, 17))
    base = jax.random.truncated_normal(first, -3.0, 3.0, (C, H), jnp.float32) / math.sqrt(C)
    scales = jnp.exp(jax.random.uniform(second, (H,), jnp.float32, math.log(0.5), math.log(2.0)))
    return base * scales[None, :]


def level_of(stream_key, dims, pieces, least, top_value):
    factor_of = 1.0
    for axis_at, shards_of in pieces:
        heights = jax.random.uniform(jax.random.fold_in(jax.random.fold_in(stream_key, 6), axis_at), (shards_of,), jnp.float32, least / len(pieces), top_value / len(pieces))
        factor_of = factor_of * jnp.repeat(jnp.exp(heights), dims[axis_at] // shards_of).reshape((-1,) + (1,) * (len(dims) - 1 - axis_at))
    return factor_of


def gaussian(key, shape, scale, most, pieces=(), dtype=jnp.bfloat16):
    entries = scale * jax.random.normal(key, shape, jnp.float32)
    if pieces:
        entries = entries * level_of(key, shape, pieces, -0.22, 0.18)
    return jnp.clip(entries, -most, most).astype(dtype)


def setup_inputs(seed: int = 0) -> dict:
    key_of = jax.random.split(jax.random.key(seed), 12)
    return {
        "pair": gaussian(key_of[0], (N, N, C), 1.0, 6.0, ((0, 4), (1, 8))),
        "norm_gain": jnp.clip(1.0 + 0.18 * jax.random.normal(key_of[1], (C,), jnp.float32), 0.1, 1.9),
        "norm_shift": gaussian(key_of[2], (C,), 0.3, 3.0, (), jnp.float32),
        "w_query": gaussian(key_of[3], (C, H * DH), 0.18, 1.0),
        "w_key": gaussian(key_of[4], (C, H * DH), C ** -0.5, 0.5),
        "w_value": gaussian(key_of[5], (C, H * DH), C ** -0.5, 0.5),
        "w_gate": gaussian(key_of[6], (C, H * DH), C ** -0.5, 0.5),
        "gate_shift": jnp.clip(jax.random.uniform(key_of[7], (H * DH,), jnp.float32, -1.0, 1.0), -1.0, 1.0),
        "w_bias": draw_w_bias(jax.random.fold_in(key_of[11], 71), 0),
        "w_out": gaussian(key_of[9], (H * DH, C), (H * DH // 4) ** -0.5, 1.0),
        "out_shift": gaussian(key_of[10], (C,), 0.5, 3.0, (), jnp.float32),
    }


def normalize(values, gain, shift):
    values = values.astype(jnp.float32)
    mean = lax.optimization_barrier(jnp.mean(values, axis=-1, keepdims=True))
    centred = values - mean
    spread = lax.optimization_barrier(jnp.mean(centred * centred, axis=-1, keepdims=True))
    return (centred * lax.rsqrt(spread + 1e-05) * gain + shift).astype(jnp.bfloat16)

def reference(pair, norm_gain, norm_shift, w_query, w_key, w_value, w_gate, gate_shift, w_bias, w_out, out_shift):
    normed = normalize(pair, norm_gain, norm_shift)
    bias = jnp.einsum('jkc,ch->hjk', normed.astype(jnp.float32), w_bias, precision=lax.Precision.HIGHEST)
    heads = w_bias.shape[1]
    inner = w_query.shape[1]
    depth = inner // heads
    seq_length = normed.shape[1]

    def one_row(pair_row):
        query = (jnp.dot(pair_row, w_query, preferred_element_type=jnp.float32) * (1.0 / math.sqrt(depth))).astype(jnp.bfloat16)
        key = jnp.dot(pair_row, w_key, preferred_element_type=jnp.float32).astype(jnp.bfloat16)
        value = jnp.dot(pair_row, w_value, preferred_element_type=jnp.float32).astype(jnp.bfloat16)
        gate = jax.nn.sigmoid(jnp.dot(pair_row, w_gate, preferred_element_type=jnp.float32) + gate_shift)
        query = query.reshape(seq_length, heads, depth).astype(jnp.float32)
        key = key.reshape(seq_length, heads, depth).astype(jnp.float32)
        value = value.reshape(seq_length, heads, depth).astype(jnp.float32)
        scores = jnp.einsum('jhd,khd->hjk', query, key) + bias
        largest = lax.optimization_barrier(jnp.max(scores, axis=2, keepdims=True))
        raised = jnp.exp(scores - largest)
        weights = (raised / lax.optimization_barrier(jnp.sum(raised, axis=2, keepdims=True))).astype(jnp.bfloat16)
        attended = jnp.einsum('hjk,khd->jhd', weights.astype(jnp.float32), value).reshape(seq_length, inner)
        gated = (gate * attended).astype(jnp.bfloat16)
        return (jnp.dot(gated, w_out, preferred_element_type=jnp.float32) + out_shift).astype(jnp.bfloat16)
    return lax.map(one_row, normed)
```

```python
import functools
import math

import jax
import jax.numpy as jnp
from jax import lax
from jax.experimental import pallas as pl
from jax.experimental.pallas import tpu as pltpu
from jax.sharding import PartitionSpec as P

F32 = jnp.float32
BF16 = jnp.bfloat16
VMEM_LIMIT = 62 * 1024 * 1024
LOG2E = math.log2(math.e)
MESH = pl.DeviceIdType.MESH


def nt_dot(a, b):
    return lax.dot_general(a, b, (((1,), (1,)), ((), ())), preferred_element_type=F32)


def layer_norm(values, gain, shift):
    mean = jnp.mean(values, axis=-1, keepdims=True)
    centred = values - mean
    spread = jnp.mean(centred * centred, axis=-1, keepdims=True)
    return (centred * lax.rsqrt(spread + 1e-05) * gain + shift).astype(BF16)


def split_bias_weights(wbt):
    high = wbt.astype(BF16)
    rest = wbt - high.astype(F32)
    mid = rest.astype(BF16)
    low = (rest - mid.astype(F32)).astype(BF16)
    return high, mid, low


def project(x, wq_ref, wkt_ref, wv_ref, q_ref, kt_ref, v_ref, heads):
    length, inner = x.shape[0], wq_ref.shape[1]
    depth = inner // heads
    query = jnp.dot(x, wq_ref[...], preferred_element_type=F32) * (1.0 / math.sqrt(depth))
    query = query.astype(BF16).astype(F32) * LOG2E
    high = query.astype(BF16)
    low = (query - high.astype(F32)).astype(BF16)
    value = jnp.dot(x, wv_ref[...], preferred_element_type=F32).astype(BF16)
    key_t = nt_dot(wkt_ref[...], x).astype(BF16)
    kt_ref[:inner] = key_t
    kt_ref[inner:] = key_t
    head_of = lax.broadcasted_iota(jnp.int32, query.shape, 1) // depth
    zero = jnp.zeros_like(high)
    for h in range(heads):
        q_ref[h, :, :inner] = jnp.where(head_of == h, high, zero)
        q_ref[h, :, inner:] = jnp.where(head_of == h, low, zero)
        v_ref[h * length : (h + 1) * length] = jnp.where(head_of == h, value, zero)


def attend_block(x, start, block, bias_ref, q_ref, kt_ref, v_ref, s_ref, w_ref, wg, gshift, group):
    pieces, heads, _, cols = bias_ref.shape
    length = kt_ref.shape[1]
    wide = max(128, cols)
    tile = max(length // 4, wide)
    for h in range(heads):
        for t in range(length // tile):
            scores = jnp.dot(
                q_ref[h, pl.ds(start, block), :],
                kt_ref[:, t * tile : (t + 1) * tile],
                preferred_element_type=F32,
            )
            for u in range(tile // wide):
                at = t * tile + u * wide
                parts = [
                    bias_ref[p, h, pl.ds(start, block), :]
                    for p in range(at // cols, (at + wide) // cols)
                ]
                bias = parts[0] if len(parts) == 1 else jnp.concatenate(parts, axis=1)
                s_ref[h, :, at : at + wide] = scores[:, u * wide : (u + 1) * wide] + bias

        def normalize_group(g, carry):
            at = pl.multiple_of(g * group, group)
            scores = s_ref[h, pl.ds(at, group), :]
            largest = jnp.max(scores, axis=1, keepdims=True)
            raised = jnp.exp2(scores - largest)
            scale = 1.0 / jnp.sum(raised, axis=1, keepdims=True)
            w_ref[pl.ds(at, group), h * length : (h + 1) * length] = (raised * scale).astype(BF16)
            return carry

        lax.fori_loop(0, block // group, normalize_group, 0, unroll=True)
    attended = jnp.dot(w_ref[...], v_ref[...], preferred_element_type=F32)
    gate = jax.nn.sigmoid(jnp.dot(x, wg, preferred_element_type=F32) + gshift)
    return (gate * attended).astype(BF16)


def fused_body(
    pair_ref, gain_ref, shift_ref, wbt_ref, wq_ref, wkt_ref, wv_ref, wg_ref, gshift_ref,
    gated_ref,
    xs_ref, xr_ref, bias_ref, q_ref, kt_ref, v_ref, s_ref, w_ref, g_ref,
    load_sem, x_send, x_recv, own_sem, b_recv, up_send, down_send, side_send, y_send, core_send,
    g_send, g_recv, g_own, *, chunk, block,
):
    n, rows, cols, channels = xs_ref.shape
    heads = bias_ref.shape[1]
    length = n * cols
    tile_rows = n * rows
    r, c = lax.axis_index("row"), lax.axis_index("col")
    row_count = lax.axis_size("row")
    lows = 2 if n % 2 == 0 else 1
    highs = n // lows
    cores = 2 if row_count % 2 == 0 else 1
    planes = row_count // cores
    z, low = c // lows, c % lows
    y, core = r // cores, r % cores
    chunks = rows // chunk

    def load(k):
        part = pl.ds(k * chunk, chunk)
        return pltpu.make_async_copy(pair_ref.at[:, part], xs_ref.at[:, part], load_sem.at[k])

    for k in range(chunks):
        load(k).start()

    high_w, mid_w, low_w = split_bias_weights(wbt_ref[...])

    def norm_chunk(k):
        load(k).wait()

        @pl.loop(0, n)
        def _(t):
            part = pl.ds(k * chunk, chunk)
            values = xs_ref[t, part].reshape(chunk * cols, channels).astype(F32)
            normed = layer_norm(values, gain_ref[...], shift_ref[...])
            xs_ref[t, part] = normed.reshape(chunk, cols, channels)
            bias = nt_dot(high_w, normed) + (nt_dot(mid_w, normed) + nt_dot(low_w, normed))
            bias = bias * LOG2E
            base = r * tile_rows + t * rows + k * chunk
            for j in range(chunk):
                bias_ref[c, :, base + j, :] = bias[:heads, j * cols : (j + 1) * cols]

    def x_copy(k, p):
        to = lax.rem(c + p, n)
        part = pl.ds(k * chunk, chunk)
        return pltpu.make_async_remote_copy(
            src_ref=xs_ref.at[to, part], dst_ref=xr_ref.at[part, c],
            send_sem=x_send.at[p, k], recv_sem=x_recv.at[p, k],
            device_id=(r, to), device_id_type=MESH,
        )

    def x_own(k):
        part = pl.ds(k * chunk, chunk)
        return pltpu.make_async_copy(xs_ref.at[c, part], xr_ref.at[part, c], own_sem.at[k])

    def send_x(k):
        for p in range(1, n):
            x_copy(k, p).start()
        x_own(k).start()

    def piece(row, col):
        return bias_ref.at[col, :, pl.ds(row * tile_rows, tile_rows), :]

    def b_copy(row, col, to, sem):
        return pltpu.make_async_remote_copy(
            src_ref=piece(row, col), dst_ref=piece(row, col), send_sem=sem,
            recv_sem=b_recv.at[row, col], device_id=to, device_id_type=MESH,
        )

    def b_wait(row, col):
        b_copy(row, col, (r, c), core_send.at[0, 0]).wait_recv()

    def up_copy(a):
        return b_copy(r, a * lows + low, (r, c + lows), up_send.at[a])

    def down_copy(a):
        return b_copy(r, a * lows + low, (r, c - lows), down_send.at[a])

    def side_copy(a):
        return b_copy(r, a * lows + low, (r, z * lows + 1 - low), side_send.at[a])

    def y_copy(q, col):
        return b_copy(r, col, (lax.rem(y + q, planes) * cores + core, c), y_send.at[q, col])

    def core_copy(plane, col):
        return b_copy(
            plane * cores + core, col, (y * cores + 1 - core, c), core_send.at[plane, col]
        )

    def forward_rows(col):
        for q in range(1, planes):
            y_copy(q, col).start()
        if cores == 2:
            core_copy(y, col).start()

    def forward_line(a):
        if lows == 2:
            side_copy(a).start()
        forward_rows(a * lows + low)

    norm_chunk(0)
    send_x(0)
    for k in range(1, chunks):
        norm_chunk(k)

    @pl.when(z < highs - 1)
    def _():
        up_copy(z).start()

    @pl.when(z > 0)
    def _():
        down_copy(z).start()

    forward_line(z)
    if chunks > 1:
        send_x(1)
    for k in range(1, highs):

        @pl.when(z - k >= 0)
        def _():
            b_wait(r, (z - k) * lows + low)

            @pl.when(z < highs - 1)
            def _():
                up_copy(z - k).start()

            forward_line(z - k)

        @pl.when(z + k < highs)
        def _():
            b_wait(r, (z + k) * lows + low)

            @pl.when(z > 0)
            def _():
                down_copy(z + k).start()

            forward_line(z + k)

    for k in range(2, chunks):
        send_x(k)
    if lows == 2:

        @pl.loop(0, highs)
        def _(a):
            col = a * lows + 1 - low
            b_wait(r, col)
            forward_rows(col)

    for q in range(1, planes):

        @pl.loop(0, n)
        def _(col):
            plane = lax.rem(y + planes - q, planes)
            b_wait(plane * cores + core, col)
            if cores == 2:
                core_copy(plane, col).start()

    if cores == 2:

        @pl.loop(0, planes * n)
        def _(i):
            b_wait((i // n) * cores + 1 - core, i % n)

    def g_copy(s, p):
        to = lax.rem(c + p, n)
        return pltpu.make_async_remote_copy(
            src_ref=g_ref.at[s, to], dst_ref=gated_ref.at[c, s],
            send_sem=g_send.at[p], recv_sem=g_recv.at[p],
            device_id=(r, to), device_id_type=MESH,
        )

    def attend_row(s):
        x = xr_ref[s].reshape(length, channels)
        project(x, wq_ref, wkt_ref, wv_ref, q_ref, kt_ref, v_ref, heads)
        groups = block // cols
        for b in range(length // block):
            part = pl.ds(b * groups, groups)
            gated = attend_block(
                xr_ref[s, part].reshape(block, channels), b * block, block, bias_ref, q_ref,
                kt_ref, v_ref, s_ref, w_ref, wg_ref[...], gshift_ref[...], 16,
            )
            g_ref[s, part] = gated.reshape(groups, cols, channels)

    @pl.loop(0, chunks)
    def _(k):
        for p in range(1, n):
            x_copy(k, p).wait_recv()
        x_own(k).wait()

        @pl.loop(0, chunk)
        def _(i):
            s = k * chunk + i
            attend_row(s)
            for p in range(1, n):
                g_copy(s, p).start()
            pltpu.make_async_copy(g_ref.at[s, c], gated_ref.at[c, s], g_own).start()

    for p in range(1, n):
        to, origin = lax.rem(c + p, n), lax.rem(c + n - p, n)
        pltpu.make_async_remote_copy(
            src_ref=g_ref.at[:, to], dst_ref=gated_ref.at[origin],
            send_sem=g_send.at[p], recv_sem=g_recv.at[p],
            device_id=(r, to), device_id_type=MESH,
        ).wait()
    pltpu.make_async_copy(g_ref.at[:, c], gated_ref.at[c], g_own).wait()

    @pl.loop(0, chunks)
    def _(k):
        for p in range(1, n):
            x_copy(k, p).wait_send()

    @pl.loop(0, highs)
    def _(a):
        if lows == 2:
            side_copy(a).wait_send()

        @pl.when((z < highs - 1) & (a <= z))
        def _():
            up_copy(a).wait_send()

        @pl.when((z > 0) & (a >= z))
        def _():
            down_copy(a).wait_send()

    @pl.loop(0, n)
    def _(col):
        for q in range(1, planes):
            y_copy(q, col).wait_send()
        if cores == 2:
            for plane in range(planes):
                core_copy(plane, col).wait_send()


def gated_attention(
    pair, norm_gain, norm_shift, w_query, w_key, w_value, w_gate, gate_shift, w_bias,
):
    n, row_count = lax.axis_size("col"), lax.axis_size("row")
    tile_rows, cols, channels = pair.shape
    rows = tile_rows // n
    length = n * cols
    heads, inner = w_bias.shape[1], w_query.shape[1]
    chunk = math.gcd(rows, 8)
    block = math.gcd(length, 512)
    wbt = jnp.pad(w_bias.T, ((0, -heads % 16), (0, 0)))
    tiled = (n, rows, cols, channels)
    highs, planes = n // (2 if n % 2 == 0 else 1), row_count // (2 if row_count % 2 == 0 else 1)
    dma = pltpu.SemaphoreType.DMA
    vmem = pl.BlockSpec(memory_space=pltpu.VMEM)
    anywhere = pl.BlockSpec(memory_space=pl.ANY)
    return pl.pallas_call(
        functools.partial(fused_body, chunk=chunk, block=block),
        in_specs=[anywhere] + [vmem] * 8,
        out_specs=anywhere,
        out_shape=jax.ShapeDtypeStruct(tiled, BF16),
        scratch_shapes=[
            pltpu.VMEM(tiled, BF16),
            pltpu.VMEM((rows, n, cols, channels), BF16),
            pltpu.VMEM((n, heads, tile_rows * row_count, cols), F32),
            pltpu.VMEM((heads, length, 2 * inner), BF16),
            pltpu.VMEM((2 * inner, length), BF16),
            pltpu.VMEM((heads * length, inner), BF16),
            pltpu.VMEM((heads, block, length), F32),
            pltpu.VMEM((block, heads * length), BF16),
            pltpu.VMEM((rows, n, cols, channels), BF16),
            dma((rows // chunk,)),
            dma((n, rows // chunk)),
            dma((n, rows // chunk)),
            dma((rows // chunk,)),
            dma((row_count, n)),
            dma((highs,)),
            dma((highs,)),
            dma((highs,)),
            dma((planes, n)),
            dma((planes, n)),
            dma((n,)),
            dma((n,)),
            dma(()),
        ],
        compiler_params=pltpu.CompilerParams(
            has_side_effects=True, vmem_limit_bytes=VMEM_LIMIT
        ),
        name="gated_attention",
    )(
        pair.reshape(tiled), norm_gain[None], norm_shift[None], wbt, w_query, w_key.T, w_value,
        w_gate, gate_shift[None],
    )


def out_body(gated_ref, wo_ref, oshift_ref, out_ref):
    rows, cols, channels = out_ref.shape
    gated = gated_ref[...].reshape(rows * cols, -1)
    update = jnp.dot(gated, wo_ref[...], preferred_element_type=F32) + oshift_ref[...]
    out_ref[...] = update.astype(BF16).reshape(rows, cols, channels)


def project_out(gated, w_out, out_shift):
    tile_rows, cols, inner = gated.shape
    channels = w_out.shape[1]
    step = math.gcd(tile_rows, 32)
    return pl.pallas_call(
        out_body,
        grid=(tile_rows // step,),
        in_specs=[
            pl.BlockSpec((step, cols, inner), lambda i: (i, 0, 0)),
            pl.BlockSpec((inner, channels), lambda i: (0, 0)),
            pl.BlockSpec((1, channels), lambda i: (0, 0)),
        ],
        out_specs=pl.BlockSpec((step, cols, channels), lambda i: (i, 0, 0)),
        out_shape=jax.ShapeDtypeStruct((tile_rows, cols, channels), BF16),
        name="project_out",
    )(gated, w_out, out_shift[None])


def on_device(
    pair, norm_gain, norm_shift, w_query, w_key, w_value, w_gate, gate_shift, w_bias, w_out,
    out_shift,
):
    gated = gated_attention(
        pair, norm_gain, norm_shift, w_query, w_key, w_value, w_gate, gate_shift, w_bias
    )
    return project_out(gated.reshape(pair.shape[:2] + (-1,)), w_out, out_shift)


def solution(mesh):
    in_specs = (P("row", "col", None),) + (P(),) * 10
    return jax.shard_map(
        on_device, mesh=mesh, in_specs=in_specs, out_specs=P("row", "col", None), check_vma=False
    )
```

```python
import functools
import math

import jax
import jax.numpy as jnp
from jax import lax
from jax.experimental import pallas as pl
from jax.experimental.pallas import tpu as pltpu
from jax.sharding import PartitionSpec as P

F32 = jnp.float32
BF16 = jnp.bfloat16
VMEM_LIMIT = 62 * 1024 * 1024
LOG2E = math.log2(math.e)
MESH = pl.DeviceIdType.MESH


def nt_dot(a, b):
    return lax.dot_general(a, b, (((1,), (1,)), ((), ())), preferred_element_type=F32)


def layer_norm(values, gain, shift):
    mean = jnp.mean(values, axis=-1, keepdims=True)
    centred = values - mean
    spread = jnp.mean(centred * centred, axis=-1, keepdims=True)
    return (centred * lax.rsqrt(spread + 1e-05) * gain + shift).astype(BF16)


def split_bias_weights(wbt):
    high = wbt.astype(BF16)
    rest = wbt - high.astype(F32)
    mid = rest.astype(BF16)
    low = (rest - mid.astype(F32)).astype(BF16)
    return high, mid, low


def project(x_ref, starts, block, wqv_ref, wkt_ref, q_ref, kt_ref, v_ref):
    heads, length, inner = v_ref.shape
    groups, cols, channels = x_ref.shape
    depth = inner // heads
    x = x_ref[...].reshape(length, channels)
    key_t = nt_dot(wkt_ref[...], x).astype(BF16)
    kt_ref[:inner] = key_t
    kt_ref[inner:] = key_t
    if len(starts) * block == length:
        both = jnp.dot(x, wqv_ref[...], preferred_element_type=F32)
        value = both[:, inner:]
        queries = [(pl.ds(0, length), both[:, :inner])]
    else:
        value = jnp.dot(x, wqv_ref[:, inner:], preferred_element_type=F32)
        queries = []
        for start in starts:
            part = x_ref[pl.ds(start // cols, block // cols)].reshape(block, channels)
            query = jnp.dot(part, wqv_ref[:, :inner], preferred_element_type=F32)
            queries.append((pl.ds(start, block), query))
    value = value.astype(BF16)
    head_of = lax.broadcasted_iota(jnp.int32, value.shape, 1) // depth
    for h in range(heads):
        v_ref[h] = jnp.where(head_of == h, value, jnp.zeros_like(value))
    for part, query in queries:
        query = query * (1.0 / math.sqrt(depth))
        query = query.astype(BF16).astype(F32) * LOG2E
        high = query.astype(BF16)
        low = (query - high.astype(F32)).astype(BF16)
        head_of = lax.broadcasted_iota(jnp.int32, high.shape, 1) // depth
        zero = jnp.zeros_like(high)
        for h in range(heads):
            q_ref[h, part, :inner] = jnp.where(head_of == h, high, zero)
            q_ref[h, part, inner:] = jnp.where(head_of == h, low, zero)


def attend(starts, block, bias_ref, q_ref, kt_ref, v_ref, s_ref, w_ref, sum_ref, group=16):
    pieces, heads, _, cols = bias_ref.shape
    length = kt_ref.shape[1]
    wide = max(128, cols)
    items = [(b, h) for b in range(len(starts)) for h in range(heads)]

    def scores_of(i):
        b, h = items[i]
        part = pl.ds(starts[b], block)
        scores = jnp.dot(q_ref[h, part, :], kt_ref[...], preferred_element_type=F32)
        for at in range(0, length, wide):
            parts = [bias_ref[p, h, part, :] for p in range(at // cols, (at + wide) // cols)]
            bias = parts[0] if len(parts) == 1 else jnp.concatenate(parts, axis=1)
            s_ref[i % 2, :, at : at + wide] = scores[:, at : at + wide] + bias

    def softmax_of(i):
        def one_group(g, carry):
            part = pl.ds(pl.multiple_of(g * group, group), group)
            scores = s_ref[i % 2, part, :]
            largest = jnp.max(scores, axis=1, keepdims=True)
            raised = jnp.exp2(scores - largest)
            scale = 1.0 / jnp.sum(raised, axis=1, keepdims=True)
            w_ref[i % 2, part, :] = (raised * scale).astype(BF16)
            return carry

        lax.fori_loop(0, block // group, one_group, 0, unroll=True)

    def values_of(i):
        b, h = items[i]
        part = jnp.dot(w_ref[i % 2], v_ref[h], preferred_element_type=F32)
        if h == 0:
            sum_ref[b] = part
        else:
            sum_ref[b] += part

    for step in range(len(items) + 2):
        if step >= 2:
            values_of(step - 2)
        if step < len(items):
            scores_of(step)
        if 1 <= step <= len(items):
            softmax_of(step - 1)


def fused_body(
    pair_ref, gain_ref, shift_ref, wbt_ref, wqv_ref, wkt_ref, wg_ref, gshift_ref,
    gated_ref,
    xs_ref, xr_ref, bias_ref, q_ref, kt_ref, v_ref, s_ref, w_ref, sum_ref, g_ref,
    load_sem, x_send, x_recv, own_sem, b_recv, up_send, down_send, side_send, y_send, core_send,
    g_send, g_recv, g_own, *, chunk,
):
    n, rows, cols, channels = xs_ref.shape
    heads = bias_ref.shape[1]
    length = n * cols
    tile_rows = n * rows
    r, c = lax.axis_index("row"), lax.axis_index("col")
    row_count = lax.axis_size("row")
    lows = 2 if n % 2 == 0 else 1
    highs = n // lows
    cores = 2 if row_count % 2 == 0 else 1
    planes = row_count // cores
    z, low = c // lows, c % lows
    y, core = r // cores, r % cores
    chunks = rows // chunk
    block = length // planes

    def load(k):
        part = pl.ds(k * chunk, chunk)
        return pltpu.make_async_copy(pair_ref.at[:, part], xs_ref.at[:, part], load_sem.at[k])

    for k in range(chunks):
        load(k).start()

    high_w, mid_w, low_w = split_bias_weights(wbt_ref[...])

    def norm_chunk(k):
        load(k).wait()

        @pl.loop(0, n)
        def _(t):
            part = pl.ds(k * chunk, chunk)
            values = xs_ref[t, part].reshape(chunk * cols, channels).astype(F32)
            normed = layer_norm(values, gain_ref[...], shift_ref[...])
            xs_ref[t, part] = normed.reshape(chunk, cols, channels)
            bias = nt_dot(high_w, normed) + (nt_dot(mid_w, normed) + nt_dot(low_w, normed))
            bias = bias * LOG2E
            base = r * tile_rows + t * rows + k * chunk
            for j in range(chunk):
                bias_ref[c, :, base + j, :] = bias[:heads, j * cols : (j + 1) * cols]

    def x_copy(k, p):
        to = lax.rem(c + p, n)
        part = pl.ds(k * chunk, chunk)
        return pltpu.make_async_remote_copy(
            src_ref=xs_ref.at[to, part], dst_ref=xr_ref.at[part, c],
            send_sem=x_send.at[p, k], recv_sem=x_recv.at[p, k],
            device_id=(r, to), device_id_type=MESH,
        )

    def x_own(k):
        part = pl.ds(k * chunk, chunk)
        return pltpu.make_async_copy(xs_ref.at[c, part], xr_ref.at[part, c], own_sem.at[k])

    def send_x(k):
        for p in range(1, n):
            x_copy(k, p).start()
        x_own(k).start()

    def piece(row, col):
        return bias_ref.at[col, :, pl.ds(row * tile_rows, tile_rows), :]

    def b_copy(row, col, to, sem):
        return pltpu.make_async_remote_copy(
            src_ref=piece(row, col), dst_ref=piece(row, col), send_sem=sem,
            recv_sem=b_recv.at[row, col], device_id=to, device_id_type=MESH,
        )

    def b_wait(row, col):
        b_copy(row, col, (r, c), core_send.at[0, 0]).wait_recv()

    def up_copy(a):
        return b_copy(r, a * lows + low, (r, c + lows), up_send.at[a])

    def down_copy(a):
        return b_copy(r, a * lows + low, (r, c - lows), down_send.at[a])

    def side_copy(a):
        return b_copy(r, a * lows + low, (r, z * lows + 1 - low), side_send.at[a])

    def y_copy(q, col):
        return b_copy(r, col, (lax.rem(y + q, planes) * cores + core, c), y_send.at[q, col])

    def core_copy(plane, col):
        return b_copy(
            plane * cores + core, col, (y * cores + 1 - core, c), core_send.at[plane, col]
        )

    def forward_rows(col):
        for q in range(1, planes):
            y_copy(q, col).start()
        if cores == 2:
            core_copy(y, col).start()

    def forward_line(a):
        if lows == 2:
            side_copy(a).start()
        forward_rows(a * lows + low)

    waiting = list(range(1, chunks))

    def send_some(count):
        for k in waiting[:count]:
            send_x(k)
        del waiting[:count]

    norm_chunk(0)
    send_x(0)
    for k in range(1, chunks):
        norm_chunk(k)

    @pl.when(z < highs - 1)
    def _():
        up_copy(z).start()

    @pl.when(z > 0)
    def _():
        down_copy(z).start()

    forward_line(z)
    send_some(1)
    for k in range(1, highs):

        @pl.when(z - k >= 0)
        def _():
            b_wait(r, (z - k) * lows + low)

            @pl.when(z < highs - 1)
            def _():
                up_copy(z - k).start()

            forward_line(z - k)

        @pl.when(z + k < highs)
        def _():
            b_wait(r, (z + k) * lows + low)

            @pl.when(z > 0)
            def _():
                down_copy(z + k).start()

            forward_line(z + k)

    send_some(2)
    if lows == 2:

        @pl.loop(0, highs)
        def _(a):
            col = a * lows + 1 - low
            b_wait(r, col)
            forward_rows(col)

    send_some(2)
    if cores == 2:

        @pl.loop(0, n)
        def _(col):
            b_wait(y * cores + 1 - core, col)

    def forward_planes():
        for q in range(1, planes):

            @pl.loop(0, n)
            def _(col):
                plane = lax.rem(y + planes - q, planes)
                b_wait(plane * cores + core, col)
                if cores == 2:
                    core_copy(plane, col).start()

    def await_planes():
        if cores == 2:
            for q in range(1, planes):

                @pl.loop(0, n)
                def _(col):
                    b_wait(lax.rem(y + q, planes) * cores + 1 - core, col)

    def g_copy(s, p):
        to = lax.rem(c + p, n)
        return pltpu.make_async_remote_copy(
            src_ref=g_ref.at[s, to], dst_ref=gated_ref.at[c, s],
            send_sem=g_send.at[p], recv_sem=g_recv.at[p],
            device_id=(r, to), device_id_type=MESH,
        )

    def attend_row(s, nth):
        starts = [pl.multiple_of(lax.rem(y + q, planes) * block, block) for q in nth]
        project(xr_ref.at[s], starts, block, wqv_ref, wkt_ref, q_ref, kt_ref, v_ref)
        attend(starts, block, bias_ref, q_ref, kt_ref, v_ref, s_ref, w_ref, sum_ref)
        groups = block // cols
        for b, start in enumerate(starts):
            first = start // cols
            x = xr_ref[s, pl.ds(first, groups)].reshape(block, channels)
            gate = jnp.dot(x, wg_ref[...], preferred_element_type=F32) + gshift_ref[...]
            gated = (jax.nn.sigmoid(gate) * sum_ref[b]).astype(BF16)
            g_ref[s, pl.ds(first, groups)] = gated.reshape(groups, cols, channels)

    def send_row(s, nth):
        groups = block // cols
        for q in nth:

            @pl.loop(0, groups)
            def _(i):
                p = lax.rem(lax.rem(y + q, planes) * groups + i + n - c, n)

                @pl.when(p > 0)
                def _():
                    g_copy(s, p).start()

                @pl.when(p == 0)
                def _():
                    pltpu.make_async_copy(g_ref.at[s, c], gated_ref.at[c, s], g_own).start()

    def attend_chunks(first, last, nth):
        @pl.loop(first * chunk, last * chunk)
        def _(s):
            attend_row(s, nth)
            send_row(s, nth)

    def await_rows(k):
        for p in range(1, n):
            x_copy(k, p).wait_recv()
        x_own(k).wait()

    early = max(1, chunks // 2)
    mine, others = (0,), tuple(range(1, planes))
    first = max(1, early // 2)

    def attend_own(start, stop):
        @pl.loop(start, stop)
        def _(k):
            await_rows(k)
            attend_chunks(k, k + 1, mine)

    attend_own(0, first)
    send_some(chunks)
    forward_planes()
    if first < early:
        attend_own(first, early)
    await_planes()
    if others:
        attend_chunks(0, early, others)

    @pl.loop(early, chunks)
    def _(k):
        await_rows(k)
        attend_chunks(k, k + 1, mine + others)

    for p in range(1, n):
        to, origin = lax.rem(c + p, n), lax.rem(c + n - p, n)
        pltpu.make_async_remote_copy(
            src_ref=g_ref.at[:, to], dst_ref=gated_ref.at[origin],
            send_sem=g_send.at[p], recv_sem=g_recv.at[p],
            device_id=(r, to), device_id_type=MESH,
        ).wait()
    pltpu.make_async_copy(g_ref.at[:, c], gated_ref.at[c], g_own).wait()

    @pl.loop(0, chunks)
    def _(k):
        for p in range(1, n):
            x_copy(k, p).wait_send()

    @pl.loop(0, highs)
    def _(a):
        if lows == 2:
            side_copy(a).wait_send()

        @pl.when((z < highs - 1) & (a <= z))
        def _():
            up_copy(a).wait_send()

        @pl.when((z > 0) & (a >= z))
        def _():
            down_copy(a).wait_send()

    @pl.loop(0, n)
    def _(col):
        for q in range(1, planes):
            y_copy(q, col).wait_send()
        if cores == 2:
            for plane in range(planes):
                core_copy(plane, col).wait_send()


def gated_attention(
    pair, norm_gain, norm_shift, w_query, w_key, w_value, w_gate, gate_shift, w_bias,
):
    n, row_count = lax.axis_size("col"), lax.axis_size("row")
    tile_rows, cols, channels = pair.shape
    rows = tile_rows // n
    length = n * cols
    heads, inner = w_bias.shape[1], w_query.shape[1]
    chunk = math.gcd(rows, 4)
    wbt = jnp.pad(w_bias.T, ((0, -heads % 16), (0, 0)))
    tiled = (n, rows, cols, channels)
    planes = row_count // (2 if row_count % 2 == 0 else 1)
    block = length // planes
    highs = n // (2 if n % 2 == 0 else 1)
    dma = pltpu.SemaphoreType.DMA
    vmem = pl.BlockSpec(memory_space=pltpu.VMEM)
    anywhere = pl.BlockSpec(memory_space=pl.ANY)
    return pl.pallas_call(
        functools.partial(fused_body, chunk=chunk),
        in_specs=[anywhere] + [vmem] * 7,
        out_specs=anywhere,
        out_shape=jax.ShapeDtypeStruct(tiled, BF16),
        scratch_shapes=[
            pltpu.VMEM(tiled, BF16),
            pltpu.VMEM((rows, n, cols, channels), BF16),
            pltpu.VMEM((n, heads, tile_rows * row_count, cols), F32),
            pltpu.VMEM((heads, length, 2 * inner), BF16),
            pltpu.VMEM((2 * inner, length), BF16),
            pltpu.VMEM((heads, length, inner), BF16),
            pltpu.VMEM((2, block, length), F32),
            pltpu.VMEM((2, block, length), BF16),
            pltpu.VMEM((planes, block, inner), F32),
            pltpu.VMEM((rows, n, cols, channels), BF16),
            dma((rows // chunk,)),
            dma((n, rows // chunk)),
            dma((n, rows // chunk)),
            dma((rows // chunk,)),
            dma((row_count, n)),
            dma((highs,)),
            dma((highs,)),
            dma((highs,)),
            dma((planes, n)),
            dma((planes, n)),
            dma((n,)),
            dma((n,)),
            dma(()),
        ],
        compiler_params=pltpu.CompilerParams(
            has_side_effects=True, vmem_limit_bytes=VMEM_LIMIT
        ),
        name="gated_attention",
    )(
        pair.reshape(tiled), norm_gain[None], norm_shift[None], wbt,
        jnp.concatenate([w_query, w_value], axis=1), w_key.T, w_gate, gate_shift[None],
    )


def out_body(gated_ref, wo_ref, oshift_ref, out_ref):
    rows, cols, channels = out_ref.shape
    gated = gated_ref[...].reshape(rows * cols, -1)
    update = jnp.dot(gated, wo_ref[...], preferred_element_type=F32) + oshift_ref[...]
    out_ref[...] = update.astype(BF16).reshape(rows, cols, channels)


def project_out(gated, w_out, out_shift):
    tile_rows, cols, inner = gated.shape
    channels = w_out.shape[1]
    step = math.gcd(tile_rows, 32)
    return pl.pallas_call(
        out_body,
        grid=(tile_rows // step,),
        in_specs=[
            pl.BlockSpec((step, cols, inner), lambda i: (i, 0, 0)),
            pl.BlockSpec((inner, channels), lambda i: (0, 0)),
            pl.BlockSpec((1, channels), lambda i: (0, 0)),
        ],
        out_specs=pl.BlockSpec((step, cols, channels), lambda i: (i, 0, 0)),
        out_shape=jax.ShapeDtypeStruct((tile_rows, cols, channels), BF16),
        name="project_out",
    )(gated, w_out, out_shift[None])


def on_device(
    pair, norm_gain, norm_shift, w_query, w_key, w_value, w_gate, gate_shift, w_bias, w_out,
    out_shift,
):
    gated = gated_attention(
        pair, norm_gain, norm_shift, w_query, w_key, w_value, w_gate, gate_shift, w_bias
    )
    return project_out(gated.reshape(pair.shape[:2] + (-1,)), w_out, out_shift)


def solution(mesh):
    in_specs = (P("row", "col", None),) + (P(),) * 10
    return jax.shard_map(
        on_device, mesh=mesh, in_specs=in_specs, out_specs=P("row", "col", None), check_vma=False
    )
```

```python
import functools
import math

import jax
import jax.numpy as jnp
from jax import lax
from jax.experimental import pallas as pl
from jax.experimental.pallas import tpu as pltpu
from jax.sharding import PartitionSpec as P

F32 = jnp.float32
BF16 = jnp.bfloat16
VMEM_LIMIT = 62 * 1024 * 1024
LOG2E = math.log2(math.e)
MESH = pl.DeviceIdType.MESH


def nt_dot(a, b):
    return lax.dot_general(a, b, (((1,), (1,)), ((), ())), preferred_element_type=F32)


def layer_norm(values, gain, shift):
    mean = jnp.mean(values, axis=-1, keepdims=True)
    centred = values - mean
    spread = jnp.mean(centred * centred, axis=-1, keepdims=True)
    return (centred * lax.rsqrt(spread + 1e-05) * gain + shift).astype(BF16)


def split_bias_weights(wbt):
    high = wbt.astype(BF16)
    rest = wbt - high.astype(F32)
    mid = rest.astype(BF16)
    low = (rest - mid.astype(F32)).astype(BF16)
    return high, mid, low


def project(x_ref, starts, block, wqv_ref, wkt_ref, q_ref, kt_ref, v_ref):
    heads, length, inner = v_ref.shape
    groups, cols, channels = x_ref.shape
    depth = inner // heads
    x = x_ref[...].reshape(length, channels)
    key_t = nt_dot(wkt_ref[...], x).astype(BF16)
    kt_ref[:inner] = key_t
    kt_ref[inner:] = key_t
    if len(starts) * block == length:
        both = jnp.dot(x, wqv_ref[...], preferred_element_type=F32)
        value = both[:, inner:]
        queries = [(pl.ds(0, length), both[:, :inner])]
    else:
        value = jnp.dot(x, wqv_ref[:, inner:], preferred_element_type=F32)
        queries = []
        for start in starts:
            part = x_ref[pl.ds(start // cols, block // cols)].reshape(block, channels)
            query = jnp.dot(part, wqv_ref[:, :inner], preferred_element_type=F32)
            queries.append((pl.ds(start, block), query))
    value = value.astype(BF16)
    head_of = lax.broadcasted_iota(jnp.int32, value.shape, 1) // depth
    for h in range(heads):
        v_ref[h] = jnp.where(head_of == h, value, jnp.zeros_like(value))
    for part, query in queries:
        query = query * (1.0 / math.sqrt(depth))
        query = query.astype(BF16).astype(F32) * LOG2E
        high = query.astype(BF16)
        low = (query - high.astype(F32)).astype(BF16)
        head_of = lax.broadcasted_iota(jnp.int32, high.shape, 1) // depth
        zero = jnp.zeros_like(high)
        for h in range(heads):
            q_ref[h, part, :inner] = jnp.where(head_of == h, high, zero)
            q_ref[h, part, inner:] = jnp.where(head_of == h, low, zero)


def attend(starts, block, bias_ref, q_ref, kt_ref, v_ref, s_ref, w_ref, sum_ref, group=16):
    pieces, heads, _, cols = bias_ref.shape
    length = kt_ref.shape[1]
    wide = max(128, cols)
    items = [(b, h) for b in range(len(starts)) for h in range(heads)]

    def scores_of(i):
        b, h = items[i]
        part = pl.ds(starts[b], block)
        scores = jnp.dot(q_ref[h, part, :], kt_ref[...], preferred_element_type=F32)
        for at in range(0, length, wide):
            parts = [bias_ref[p, h, part, :] for p in range(at // cols, (at + wide) // cols)]
            bias = parts[0] if len(parts) == 1 else jnp.concatenate(parts, axis=1)
            s_ref[i % 2, :, at : at + wide] = scores[:, at : at + wide] + bias

    def softmax_of(i):
        def one_group(g, carry):
            part = pl.ds(pl.multiple_of(g * group, group), group)
            scores = s_ref[i % 2, part, :]
            largest = jnp.max(scores, axis=1, keepdims=True)
            raised = jnp.exp2(scores - largest)
            scale = 1.0 / jnp.sum(raised, axis=1, keepdims=True)
            w_ref[i % 2, part, :] = (raised * scale).astype(BF16)
            return carry

        lax.fori_loop(0, block // group, one_group, 0, unroll=True)

    def values_of(i):
        b, h = items[i]
        part = jnp.dot(w_ref[i % 2], v_ref[h], preferred_element_type=F32)
        if h == 0:
            sum_ref[b] = part
        else:
            sum_ref[b] += part

    for step in range(len(items) + 2):
        if step >= 2:
            values_of(step - 2)
        if step < len(items):
            scores_of(step)
        if 1 <= step <= len(items):
            softmax_of(step - 1)


def fused_body(
    pair_ref, gain_ref, shift_ref, wbt_ref, wq_ref, wk_ref, wv_ref, wg_ref, gshift_ref,
    gated_ref,
    wqv_ref, wkt_ref, xs_ref, xr_ref, bias_ref, q_ref, kt_ref, v_ref, s_ref, w_ref, sum_ref, g_ref,
    load_sem, x_send, x_recv, own_sem, b_recv, up_send, down_send, side_send, y_send, core_send,
    g_send, g_recv, g_own, *, chunk,
):
    n, rows, cols, channels = xs_ref.shape
    heads = bias_ref.shape[1]
    length = n * cols
    tile_rows = n * rows
    r, c = lax.axis_index("row"), lax.axis_index("col")
    row_count = lax.axis_size("row")
    lows = 2 if n % 2 == 0 else 1
    highs = n // lows
    cores = 2 if row_count % 2 == 0 else 1
    planes = row_count // cores
    z, low = c // lows, c % lows
    y, core = r // cores, r % cores
    chunks = rows // chunk
    block = length // planes

    def load(k):
        part = pl.ds(k * chunk, chunk)
        return pltpu.make_async_copy(pair_ref.at[:, part], xs_ref.at[:, part], load_sem.at[k])

    for k in range(chunks):
        load(k).start()

    high_w, mid_w, low_w = split_bias_weights(wbt_ref[...])

    def norm_chunk(k):
        load(k).wait()

        @pl.loop(0, n)
        def _(t):
            part = pl.ds(k * chunk, chunk)
            values = xs_ref[t, part].reshape(chunk * cols, channels).astype(F32)
            normed = layer_norm(values, gain_ref[...], shift_ref[...])
            xs_ref[t, part] = normed.reshape(chunk, cols, channels)
            bias = nt_dot(high_w, normed) + (nt_dot(mid_w, normed) + nt_dot(low_w, normed))
            bias = bias * LOG2E
            base = r * tile_rows + t * rows + k * chunk
            for j in range(chunk):
                bias_ref[c, :, base + j, :] = bias[:heads, j * cols : (j + 1) * cols]

    def x_copy(k, p):
        to = lax.rem(c + p, n)
        part = pl.ds(k * chunk, chunk)
        return pltpu.make_async_remote_copy(
            src_ref=xs_ref.at[to, part], dst_ref=xr_ref.at[part, c],
            send_sem=x_send.at[p, k], recv_sem=x_recv.at[p, k],
            device_id=(r, to), device_id_type=MESH,
        )

    def x_own(k):
        part = pl.ds(k * chunk, chunk)
        return pltpu.make_async_copy(xs_ref.at[c, part], xr_ref.at[part, c], own_sem.at[k])

    def send_x(k):
        for p in range(1, n):
            x_copy(k, p).start()
        x_own(k).start()

    def piece(row, col):
        return bias_ref.at[col, :, pl.ds(row * tile_rows, tile_rows), :]

    def b_copy(row, col, to, sem):
        return pltpu.make_async_remote_copy(
            src_ref=piece(row, col), dst_ref=piece(row, col), send_sem=sem,
            recv_sem=b_recv.at[row, col], device_id=to, device_id_type=MESH,
        )

    def b_wait(row, col):
        b_copy(row, col, (r, c), core_send.at[0, 0]).wait_recv()

    def up_copy(a):
        return b_copy(r, a * lows + low, (r, c + lows), up_send.at[a])

    def down_copy(a):
        return b_copy(r, a * lows + low, (r, c - lows), down_send.at[a])

    def side_copy(a):
        return b_copy(r, a * lows + low, (r, z * lows + 1 - low), side_send.at[a])

    def y_copy(q, col):
        return b_copy(r, col, (lax.rem(y + q, planes) * cores + core, c), y_send.at[q, col])

    def core_copy(plane, col):
        return b_copy(
            plane * cores + core, col, (y * cores + 1 - core, c), core_send.at[plane, col]
        )

    def forward_rows(col):
        for q in range(1, planes):
            y_copy(q, col).start()
        if cores == 2:
            core_copy(y, col).start()

    def forward_line(a):
        if lows == 2:
            side_copy(a).start()
        forward_rows(a * lows + low)

    waiting = list(range(1, chunks))

    def send_some(count):
        for k in waiting[:count]:
            send_x(k)
        del waiting[:count]

    norm_chunk(0)
    send_x(0)
    inner = wq_ref.shape[1]
    wqv_ref[:, :inner] = wq_ref[...]
    wqv_ref[:, inner:] = wv_ref[...]
    wkt_ref[...] = wk_ref[...].T
    for k in range(1, chunks):
        norm_chunk(k)

    @pl.when(z < highs - 1)
    def _():
        up_copy(z).start()

    @pl.when(z > 0)
    def _():
        down_copy(z).start()

    forward_line(z)
    send_some(1)
    for k in range(1, highs):

        @pl.when(z - k >= 0)
        def _():
            b_wait(r, (z - k) * lows + low)

            @pl.when(z < highs - 1)
            def _():
                up_copy(z - k).start()

            forward_line(z - k)

        @pl.when(z + k < highs)
        def _():
            b_wait(r, (z + k) * lows + low)

            @pl.when(z > 0)
            def _():
                down_copy(z + k).start()

            forward_line(z + k)

    send_some(2)
    if lows == 2:

        @pl.loop(0, highs)
        def _(a):
            col = a * lows + 1 - low
            b_wait(r, col)
            forward_rows(col)

    send_some(2)
    if cores == 2:

        @pl.loop(0, n)
        def _(col):
            b_wait(y * cores + 1 - core, col)

    def forward_planes():
        for q in range(1, planes):

            @pl.loop(0, n)
            def _(col):
                plane = lax.rem(y + planes - q, planes)
                b_wait(plane * cores + core, col)
                if cores == 2:
                    core_copy(plane, col).start()

    def await_planes():
        if cores == 2:
            for q in range(1, planes):

                @pl.loop(0, n)
                def _(col):
                    b_wait(lax.rem(y + q, planes) * cores + 1 - core, col)

    def g_copy(s, p):
        to = lax.rem(c + p, n)
        return pltpu.make_async_remote_copy(
            src_ref=g_ref.at[s, to], dst_ref=gated_ref.at[c, s],
            send_sem=g_send.at[p], recv_sem=g_recv.at[p],
            device_id=(r, to), device_id_type=MESH,
        )

    def attend_row(s, nth):
        starts = [pl.multiple_of(lax.rem(y + q, planes) * block, block) for q in nth]
        project(xr_ref.at[s], starts, block, wqv_ref, wkt_ref, q_ref, kt_ref, v_ref)
        attend(starts, block, bias_ref, q_ref, kt_ref, v_ref, s_ref, w_ref, sum_ref)
        groups = block // cols
        for b, start in enumerate(starts):
            first = start // cols
            x = xr_ref[s, pl.ds(first, groups)].reshape(block, channels)
            gate = jnp.dot(x, wg_ref[...], preferred_element_type=F32) + gshift_ref[...]
            gated = (jax.nn.sigmoid(gate) * sum_ref[b]).astype(BF16)
            g_ref[s, pl.ds(first, groups)] = gated.reshape(groups, cols, channels)

    def send_row(s, nth):
        groups = block // cols
        for q in nth:

            @pl.loop(0, groups)
            def _(i):
                p = lax.rem(lax.rem(y + q, planes) * groups + i + n - c, n)

                @pl.when(p > 0)
                def _():
                    g_copy(s, p).start()

                @pl.when(p == 0)
                def _():
                    pltpu.make_async_copy(g_ref.at[s, c], gated_ref.at[c, s], g_own).start()

    def attend_chunks(first, last, nth):
        @pl.loop(first * chunk, last * chunk)
        def _(s):
            attend_row(s, nth)
            send_row(s, nth)

    def await_rows(k):
        for p in range(1, n):
            x_copy(k, p).wait_recv()
        x_own(k).wait()

    early = max(1, chunks // 2)
    mine, others = (0,), tuple(range(1, planes))
    first = max(1, early // 2)

    def attend_own(start, stop):
        @pl.loop(start, stop)
        def _(k):
            await_rows(k)
            attend_chunks(k, k + 1, mine)

    attend_own(0, first)
    send_some(chunks)
    forward_planes()
    if first < early:
        attend_own(first, early)
    await_planes()
    if others:
        attend_chunks(0, early, others)

    @pl.loop(early, chunks)
    def _(k):
        await_rows(k)
        attend_chunks(k, k + 1, mine + others)

    for p in range(1, n):
        to, origin = lax.rem(c + p, n), lax.rem(c + n - p, n)
        pltpu.make_async_remote_copy(
            src_ref=g_ref.at[:, to], dst_ref=gated_ref.at[origin],
            send_sem=g_send.at[p], recv_sem=g_recv.at[p],
            device_id=(r, to), device_id_type=MESH,
        ).wait()
    pltpu.make_async_copy(g_ref.at[:, c], gated_ref.at[c], g_own).wait()

    @pl.loop(0, chunks)
    def _(k):
        for p in range(1, n):
            x_copy(k, p).wait_send()

    @pl.loop(0, highs)
    def _(a):
        if lows == 2:
            side_copy(a).wait_send()

        @pl.when((z < highs - 1) & (a <= z))
        def _():
            up_copy(a).wait_send()

        @pl.when((z > 0) & (a >= z))
        def _():
            down_copy(a).wait_send()

    @pl.loop(0, n)
    def _(col):
        for q in range(1, planes):
            y_copy(q, col).wait_send()
        if cores == 2:
            for plane in range(planes):
                core_copy(plane, col).wait_send()


def gated_attention(
    pair, norm_gain, norm_shift, w_query, w_key, w_value, w_gate, gate_shift, w_bias,
):
    n, row_count = lax.axis_size("col"), lax.axis_size("row")
    tile_rows, cols, channels = pair.shape
    rows = tile_rows // n
    length = n * cols
    heads, inner = w_bias.shape[1], w_query.shape[1]
    chunk = math.gcd(rows, 4)
    tiled = (n, rows, cols, channels)
    planes = row_count // (2 if row_count % 2 == 0 else 1)
    block = length // planes
    highs = n // (2 if n % 2 == 0 else 1)
    dma = pltpu.SemaphoreType.DMA
    vmem = pl.BlockSpec(memory_space=pltpu.VMEM)
    anywhere = pl.BlockSpec(memory_space=pl.ANY)
    return pl.pallas_call(
        functools.partial(fused_body, chunk=chunk),
        in_specs=[anywhere] + [vmem] * 8,
        out_specs=anywhere,
        out_shape=jax.ShapeDtypeStruct(tiled, BF16),
        scratch_shapes=[
            pltpu.VMEM((channels, 2 * inner), BF16),
            pltpu.VMEM((inner, channels), BF16),
            pltpu.VMEM(tiled, BF16),
            pltpu.VMEM((rows, n, cols, channels), BF16),
            pltpu.VMEM((n, heads, tile_rows * row_count, cols), F32),
            pltpu.VMEM((heads, length, 2 * inner), BF16),
            pltpu.VMEM((2 * inner, length), BF16),
            pltpu.VMEM((heads, length, inner), BF16),
            pltpu.VMEM((2, block, length), F32),
            pltpu.VMEM((2, block, length), BF16),
            pltpu.VMEM((planes, block, inner), F32),
            pltpu.VMEM((rows, n, cols, channels), BF16),
            dma((rows // chunk,)),
            dma((n, rows // chunk)),
            dma((n, rows // chunk)),
            dma((rows // chunk,)),
            dma((row_count, n)),
            dma((highs,)),
            dma((highs,)),
            dma((highs,)),
            dma((planes, n)),
            dma((planes, n)),
            dma((n,)),
            dma((n,)),
            dma(()),
        ],
        compiler_params=pltpu.CompilerParams(
            has_side_effects=True, vmem_limit_bytes=VMEM_LIMIT
        ),
        name="gated_attention",
    )(
        pair.reshape(tiled), norm_gain[None], norm_shift[None], w_bias.T, w_query,
        w_key, w_value, w_gate, gate_shift[None],
    )


def out_body(gated_ref, wo_ref, oshift_ref, out_ref):
    rows, cols, channels = out_ref.shape
    gated = gated_ref[...].reshape(rows * cols, -1)
    update = jnp.dot(gated, wo_ref[...], preferred_element_type=F32) + oshift_ref[...]
    out_ref[...] = update.astype(BF16).reshape(rows, cols, channels)


def project_out(gated, w_out, out_shift):
    tile_rows, cols, inner = gated.shape
    channels = w_out.shape[1]
    step = math.gcd(tile_rows, 64)
    return pl.pallas_call(
        out_body,
        grid=(tile_rows // step,),
        in_specs=[
            pl.BlockSpec((step, cols, inner), lambda i: (i, 0, 0)),
            pl.BlockSpec((inner, channels), lambda i: (0, 0)),
            pl.BlockSpec((1, channels), lambda i: (0, 0)),
        ],
        out_specs=pl.BlockSpec((step, cols, channels), lambda i: (i, 0, 0)),
        out_shape=jax.ShapeDtypeStruct((tile_rows, cols, channels), BF16),
        compiler_params=pltpu.CompilerParams(vmem_limit_bytes=VMEM_LIMIT),
        name="project_out",
    )(gated, w_out, out_shift[None])


def on_device(
    pair, norm_gain, norm_shift, w_query, w_key, w_value, w_gate, gate_shift, w_bias, w_out,
    out_shift,
):
    gated = gated_attention(
        pair, norm_gain, norm_shift, w_query, w_key, w_value, w_gate, gate_shift, w_bias
    )
    return project_out(gated.reshape(pair.shape[:2] + (-1,)), w_out, out_shift)


def solution(mesh):
    in_specs = (P("row", "col", None),) + (P(),) * 10
    return jax.shard_map(
        on_device, mesh=mesh, in_specs=in_specs, out_specs=P("row", "col", None), check_vma=False
    )
```
